256 devices in a mesh: ctx: 64 (over x_hi, y, z), tp: 4 (over x_lo, core).
Axes of the slice: x: 4 (x_hi: 2, x_lo: 2; x = x_hi * 2 + x_lo), y: 4, z: 8, core: 2. Of those that a mesh axis runs over, the one named last changes fastest.
Arguments:
- hidden: bfloat16 [16384, 2048], P('ctx', 'tp'), may hold values from -6 to 6
- norm_gain_a: float32 [2048], replicated, may hold values from 0.5 to 1.5
- in_weight_a: bfloat16 [3, 2048, 2048], P(None, 'ctx', 'tp'), may hold values from -0.125 to 0.125
- mr_filter: bfloat16 [128, 128], P('tp'), may hold values from -0.5 to 0.5
- out_weight_a: bfloat16 [2048, 2048], P('tp', 'ctx'), may hold values from -0.125 to 0.125
- norm_gain_b: float32 [2048], replicated, may hold values from 0.5 to 1.5
- in_weight_b: bfloat16 [3, 2048, 2048], P(None, 'ctx', 'tp'), may hold values from -0.125 to 0.125
- li_rate: float32 [128, 16], P('tp'), may hold values from 6.1035156e-06 to 0.0333333333
- li_residue: float32 [128, 16], P('tp'), may hold values from -3 to 3
- out_weight_b: bfloat16 [2048, 2048], P('tp', 'ctx'), may hold values from -0.125 to 0.125
Outputs:
- mixed: bfloat16 [16384, 2048], P('ctx', 'tp')
- gated_medium: bfloat16 [2048, 16384], P('tp', 'ctx')
- gated_long: bfloat16 [2048, 16384], P('tp', 'ctx')
The draws below stay inside these ranges and needn't reach their ends.
All inputs are finite; a program needn't handle non-finite values.
Results may differ from the reference program's by a relative error of at most 0.02.
Values may be sent and summed in bfloat16 or wider, within the bound.
No kernel may reach another device: no remote copies, remote signals or barrier semaphores. Data moves between devices by JAX's collectives and lax.ppermute only.
A program may use at most 64 MiB of HBM per device.

```python
import math
import jax
import jax.numpy as jnp
from jax import lax

D = 2048
CH = 2048
GROUP = 16
TAPS = 128
MODES = 16
SEQ = 16384
GROUPS = 128


def draw_li_rate(key, part):
    share_key, slow_key, fast_key = jax.random.split(jax.random.fold_in(key, 7), 3)
    slow_share = 0.5
    picked = jax.random.uniform(share_key, (GROUPS, MODES)) < slow_share
    slow_rate = jnp.exp(jax.random.uniform(slow_key, (GROUPS, MODES), minval=math.log(0.1 / SEQ), maxval=math.log(2.0 / SEQ)))
    fast_rate = jnp.exp(jax.random.uniform(fast_key, (GROUPS, MODES), minval=math.log(1.0 / 50.0), maxval=math.log(1.0 / 30.0)))
    return jnp.where(picked, slow_rate, fast_rate).astype(jnp.float32)


def levels(rng, extent, pieces, least, top_value):
    def one(dim, shards_of):
        draws = jax.random.uniform(jax.random.fold_in(jax.random.fold_in(rng, 6), dim), (shards_of,), jnp.float32, least / len(pieces), top_value / len(pieces))
        return jnp.repeat(jnp.exp(draws), extent[dim] // shards_of).reshape((-1,) + (1,) * (len(extent) - dim - 1))

    level = one(*pieces[0])
    for cut in pieces[1:]:
        level = level * one(*cut)
    return level


def bell_draw(key, extent, deviation, limit, shards=(), held_as=jnp.bfloat16):
    array = deviation * jax.random.normal(key, extent, jnp.float32)
    if shards:
        array = array * levels(key, extent, shards, -0.22, 0.18)
    return jnp.clip(array, -limit, limit).astype(held_as)


def setup_inputs(seed: int = 0) -> dict:
    arg_keys = jax.random.split(jax.random.key(seed), 11)
    return {
        "hidden": bell_draw(arg_keys[0], (SEQ, D), 1.0, 6.0, ((0, 64), (1, 4))),
        "norm_gain_a": jnp.clip(1.0 + 0.1 * jax.random.normal(arg_keys[1], (D,), jnp.float32), 0.5, 1.5),
        "in_weight_a": bell_draw(arg_keys[2], (3, D, CH), D ** -0.5, 0.125, ((1, 64), (2, 4))),
        "mr_filter": bell_draw(arg_keys[3], (GROUPS, TAPS), TAPS ** -0.5, 0.5, ((0, 4),)),
        "out_weight_a": bell_draw(arg_keys[4], (CH, D), CH ** -0.5, 0.125, ((0, 4), (1, 64))),
        "norm_gain_b": jnp.clip(1.0 + 0.1 * jax.random.normal(arg_keys[5], (D,), jnp.float32), 0.5, 1.5),
        "in_weight_b": bell_draw(arg_keys[6], (3, D, CH), D ** -0.5, 0.125, ((1, 64), (2, 4))),
        "li_rate": draw_li_rate(jax.random.fold_in(arg_keys[10], 71), 0),
        "li_residue": bell_draw(arg_keys[8], (GROUPS, MODES), 0.5, 3.0, ((0, 4),), jnp.float32),
        "out_weight_b": bell_draw(arg_keys[9], (CH, D), CH ** -0.5, 0.125, ((0, 4), (1, 64))),
    }


def normalize(values, gain):
    widened = values.astype(jnp.float32)
    factor = lax.rsqrt(lax.optimization_barrier(jnp.mean(widened * widened, axis=1, keepdims=True)) + 1e-06)
    return (widened * factor * gain).astype(jnp.bfloat16)

def layer_inputs(values, gain, weight):
    normed = normalize(values, gain)
    first = jnp.dot(normed, weight[0], preferred_element_type=jnp.float32)
    gating = jnp.dot(normed, weight[1], preferred_element_type=jnp.float32)
    second = jnp.dot(normed, weight[2], preferred_element_type=jnp.float32)
    return (gating, (first * second).astype(jnp.bfloat16))

def causal_conv(values, filters):
    length = values.shape[0]
    padded_len = 2 * length
    grouped = values.reshape(length, GROUPS, GROUP).transpose(1, 0, 2)

    def one_group(pair):
        group_values, group_filter = pair
        spectrum = jnp.fft.rfft(group_values, n=padded_len, axis=0)
        response = jnp.fft.rfft(group_filter, n=padded_len)
        return jnp.fft.irfft(spectrum * response[:, None], n=padded_len, axis=0)[:length].astype(jnp.float32)
    result = lax.map(one_group, (grouped, filters))
    return result.transpose(1, 0, 2).reshape(length, GROUPS * GROUP)

def reference(hidden, norm_gain_a, in_weight_a, mr_filter, out_weight_a, norm_gain_b, in_weight_b, li_rate, li_residue, out_weight_b):
    gate_first, medium_in = layer_inputs(hidden, norm_gain_a, in_weight_a)
    medium = causal_conv(medium_in.astype(jnp.float32), mr_filter.astype(jnp.float32))
    gated_medium = (gate_first * medium).astype(jnp.bfloat16)
    after_a = (hidden.astype(jnp.float32) + jnp.dot(gated_medium, out_weight_a, preferred_element_type=jnp.float32)).astype(jnp.bfloat16)
    gate_second, long_in = layer_inputs(after_a, norm_gain_b, in_weight_b)
    offsets = jnp.arange(SEQ, dtype=jnp.float32)
    mode_weight = li_residue * jnp.sqrt(2.0 * li_rate)
    long_filter = lax.optimization_barrier(jnp.sum(mode_weight[:, :, None] * jnp.exp(-li_rate[:, :, None] * offsets), axis=1))
    long_out = causal_conv(long_in.astype(jnp.float32), long_filter)
    gated_long = (gate_second * long_out).astype(jnp.bfloat16)
    mixed = (after_a.astype(jnp.float32) + jnp.dot(gated_long, out_weight_b, preferred_element_type=jnp.float32)).astype(jnp.bfloat16)
    return (mixed, gated_medium.T, gated_long.T)
```

```python
import jax
import jax.numpy as jnp
from jax import lax
from jax.sharding import Mesh
from jax.sharding import PartitionSpec as P

GROUP = 16
TAPS = 128
CTX = ("xh", "y", "z")
TP = ("xl", "co")
RING = ("xh", "xl")
BF = jnp.bfloat16
F32 = jnp.float32


def from_everyone(shard, axis):
    copies = jnp.broadcast_to(shard, (lax.axis_size(axis), *shard.shape))
    return lax.all_to_all(copies, axis, split_axis=0, concat_axis=0, tiled=True)


def swap_core(value):
    return lax.ppermute(value, "co", [(0, 1), (1, 0)])


def gather_weight(w):
    k, rows, cols = w.shape
    halves = jnp.moveaxis(w.reshape(k, rows, 2, cols // 2), 2, 0)
    both = lax.all_to_all(halves, "xh", split_axis=0, concat_axis=0, tiled=True)
    return from_everyone(from_everyone(both, "z"), "y")


def gather_tokens(block):
    mine = from_everyone(block, RING)
    theirs = swap_core(mine)
    core = lax.axis_index("co")
    pair = jnp.stack([jnp.where(core == 0, mine, theirs), jnp.where(core == 0, theirs, mine)])
    tokens, feats = block.shape
    pair = pair.reshape(2, 2, 2, tokens, feats)
    return pair.transpose(1, 3, 2, 0, 4).reshape(2 * tokens, 4 * feats)


def normalize(values, gain):
    widened = values.astype(F32)
    factor = lax.rsqrt(jnp.mean(widened * widened, axis=1, keepdims=True) + 1e-06)
    return (widened * factor * gain).astype(BF)


def layer_inputs(gathered, gain, weight):
    normed = normalize(gathered, gain)
    k = weight.shape[3]
    flat = weight.transpose(3, 2, 0, 1, 4, 5).reshape(k, -1, weight.shape[-1])
    projected = jnp.einsum("knc,tn->kct", flat, normed, preferred_element_type=F32)
    return projected[1], (projected[0] * projected[2]).astype(BF)


def out_project(gated, weight):
    chans = gated.shape[0]
    flat = weight.transpose(3, 2, 0, 1, 4, 5).reshape(2, 2, -1, chans)
    core = lax.axis_index("co")
    keep = lax.dynamic_index_in_dim(flat, core, 1, keepdims=False)
    send = lax.dynamic_index_in_dim(flat, 1 - core, 1, keepdims=False)
    dims = "cbt,xnc->bxtn"
    g = gated.reshape(chans, 2, -1)
    away = jnp.einsum(dims, g, send, preferred_element_type=F32).astype(BF)
    got = swap_core(away)
    here = jnp.einsum(dims, g, keep, preferred_element_type=F32)
    summed = (here + got.astype(F32)).astype(BF)
    summed = summed.reshape(4, *summed.shape[2:])
    parts = lax.all_to_all(summed, RING, 0, 0, tiled=True)
    return jnp.sum(parts.astype(F32), axis=0)


def toeplitz_rows(filters):
    group_count, tap_count = filters.shape
    padded_filter = jnp.concatenate(
        [
            jnp.zeros((group_count, 1), filters.dtype),
            filters[:, ::-1],
            jnp.zeros((group_count, tap_count), filters.dtype),
        ],
        axis=1,
    )
    tiled = jnp.tile(padded_filter, (1, tap_count))[:, : tap_count * 2 * tap_count]
    return tiled.reshape(group_count, tap_count, 2 * tap_count)


def medium_conv(medium_in, rows):
    chans, tokens = medium_in.shape
    per = tokens // 2
    blocks = medium_in.reshape(chans, 2, per)
    count = lax.axis_size(("y", "z"))
    rim = lax.ppermute(blocks[:, :, per - TAPS :], ("y", "z"), [(i, (i + 1) % count) for i in range(count)])
    first = lax.axis_index(("y", "z")) == 0
    wrapped = jnp.concatenate([jnp.zeros_like(rim[:, :1]), rim[:, :1]], axis=1)
    rim = jnp.where(first, wrapped, rim)
    extended = jnp.concatenate([rim, blocks], axis=2)
    groups = chans // GROUP
    n = per // TAPS
    grouped = extended.reshape(groups, GROUP, 2, n + 1, TAPS)
    windows = jnp.concatenate([grouped[:, :, :, :-1], grouped[:, :, :, 1:]], axis=4)
    result = jnp.einsum("gts,gkhbs->gkhbt", rows, windows, preferred_element_type=F32)
    return result.reshape(chans, tokens)


def long_conv(long_in, rates, residues):
    chans, tokens = long_in.shape
    per = tokens // 2
    groups = chans // GROUP
    values = long_in.reshape(groups, GROUP, 2, per)
    offsets = jnp.arange(per, dtype=F32)
    mode_weight = residues * jnp.sqrt(2.0 * rates)
    decays = jnp.exp(-rates[:, :, None] * offsets)
    impulse = jnp.sum(mode_weight[:, :, None] * decays, axis=1)
    rows = toeplitz_rows(impulse.astype(BF))[:, :, per:]
    to_end = decays[:, :, ::-1].astype(BF)
    ends = jnp.einsum("gms,gkhs->gmkh", to_end, values, preferred_element_type=F32)
    y = lax.axis_index("y").astype(F32)
    z = lax.axis_index("z").astype(F32)
    zs = lax.axis_size("z")
    ys = lax.axis_size("y")

    def weights(count, here, span):
        idx = jnp.arange(count, dtype=F32)[:, None, None]
        gap = here - 1.0 - idx
        before = jnp.where(gap >= 0, jnp.exp(-rates * (span * jnp.maximum(gap, 0.0))), 0.0)
        total = jnp.exp(-rates * (span * (count - 1.0 - idx)))
        return before[..., None, None], total[..., None, None]

    by_z = from_everyone(ends.astype(BF), "z").astype(F32)
    before, total = weights(zs, z, float(per))
    row_before = jnp.sum(before * by_z, axis=0)
    row_total = jnp.sum(total * by_z, axis=0)
    by_y = from_everyone(row_total.astype(BF), "y").astype(F32)
    before, total = weights(ys, y, float(per * zs))
    half_before = jnp.sum(before * by_y, axis=0)
    half_total = jnp.sum(total * by_y, axis=0)
    carry = jnp.exp(-rates * (per * zs * y))[:, :, None]
    first_half = half_before[..., 0]
    second_half = half_before[..., 1] + carry * half_total[..., 0]
    entering = row_before + jnp.exp(-rates * (per * z))[:, :, None, None] * jnp.stack([first_half, second_half], axis=-1)
    within = jnp.einsum("gts,gkhs->gkht", rows, values, preferred_element_type=F32)
    from_start = (mode_weight * jnp.exp(-rates))[:, :, None] * decays
    carried = jnp.einsum("gmt,gmkh->gkht", from_start.astype(BF), entering.astype(BF), preferred_element_type=F32)
    return (within + carried).reshape(chans, tokens)


def placed(gated):
    chans, tokens = gated.shape
    blocks = jnp.moveaxis(gated.reshape(chans, 2, tokens // 2), 1, 0)
    got = lax.all_to_all(blocks, "xh", split_axis=0, concat_axis=0, tiled=True)
    return got.reshape(2 * chans, tokens // 2)


def per_device(hidden, gain_a, in_a, mr_filter, out_a, gain_b, in_b, li_rate, li_residue, out_b):
    half = lax.axis_index("xh")
    mr = lax.dynamic_slice_in_dim(mr_filter, half * (mr_filter.shape[0] // 2), mr_filter.shape[0] // 2, 0)
    rates = lax.dynamic_slice_in_dim(li_rate, half * (li_rate.shape[0] // 2), li_rate.shape[0] // 2, 0)
    residues = lax.dynamic_slice_in_dim(li_residue, half * (li_residue.shape[0] // 2), li_residue.shape[0] // 2, 0)
    w_in_a = gather_weight(in_a)
    gathered = gather_tokens(hidden)
    w_out_a = gather_weight(out_a.T[None])
    w_in_b = gather_weight(in_b)
    w_out_b = gather_weight(out_b.T[None])
    gate, medium_in = layer_inputs(gathered, gain_a, w_in_a)
    gated = (gate * medium_conv(medium_in, toeplitz_rows(mr))).astype(BF)
    gated_medium = placed(gated)
    after_a = (hidden.astype(F32) + out_project(gated, w_out_a)).astype(BF)
    gathered_b = gather_tokens(after_a)
    gate_b, long_in = layer_inputs(gathered_b, gain_b, w_in_b)
    gated_b = (gate_b * long_conv(long_in, rates, residues)).astype(BF)
    gated_long = placed(gated_b)
    mixed = (after_a.astype(F32) + out_project(gated_b, w_out_b)).astype(BF)
    return mixed, gated_medium, gated_long


def solution(mesh):
    split = Mesh(mesh.devices.reshape(2, 4, 8, 2, 2), ("xh", "y", "z", "xl", "co"))
    in_specs = (
        P(CTX, TP),
        P(),
        P(None, CTX, TP),
        P(TP, None),
        P(TP, CTX),
        P(),
        P(None, CTX, TP),
        P(TP, None),
        P(TP, None),
        P(TP, CTX),
    )
    out_specs = (P(CTX, TP), P(TP, CTX), P(TP, CTX))
    return jax.shard_map(per_device, mesh=split, in_specs=in_specs, out_specs=out_specs, check_vma=False)
```

```python
import functools

import jax
import jax.numpy as jnp
from jax import lax
from jax.experimental import pallas as pl
from jax.experimental.pallas import tpu as pltpu
from jax.sharding import Mesh
from jax.sharding import PartitionSpec as P

GROUP = 16
TAPS = 128
CTX = ("xh", "y", "z")
TP = ("xl", "co")
RING = ("xh", "xl")
ROWS = ("y", "z")
BF = jnp.bfloat16
F32 = jnp.float32
SIZES = {"xh": 2, "y": 4, "z": 8, "xl": 2, "co": 2}


ANY = pl.BlockSpec(memory_space=pl.ANY)
VM = pl.BlockSpec(memory_space=pltpu.VMEM)
SM = pl.BlockSpec(memory_space=pltpu.SMEM)


def shift(value, axis, steps):
    n = SIZES[axis]
    return lax.ppermute(value, axis, [(i, (i + steps) % n) for i in range(n)])


def flip(value, axis, bit):
    return lax.ppermute(value, axis, [(i, i ^ bit) for i in range(SIZES[axis])])


def ring_shift(value, steps):
    return lax.ppermute(value, RING, [(i, (i + steps) % 4) for i in range(4)])


def from_everyone(shard, axis):
    copies = jnp.broadcast_to(shard, (lax.axis_size(axis), *shard.shape))
    return lax.all_to_all(copies, axis, split_axis=0, concat_axis=0, tiled=True)


def column_halves(in_w, out_w, half):
    both = jnp.concatenate([in_w, out_w.T[None]], axis=0)
    k, rows, cols = both.shape
    own = lax.dynamic_slice_in_dim(both, half * (cols // 2), cols // 2, 2)
    away = lax.dynamic_slice_in_dim(both, (1 - half) * (cols // 2), cols // 2, 2)
    return own, away


def gather_first(own, away):
    got = shift(away, "xh", 1)
    ys = [own, shift(own, "y", 1), shift(own, "y", 2), shift(own, "y", -1)]
    bundle = jnp.stack(ys)
    forth, back = [bundle], [bundle]
    for _ in range(3):
        forth.append(shift(forth[-1], "z", 1))
        back.append(shift(back[-1], "z", -1))
    far_a = shift(forth[-1][:2], "z", 1)
    far_b = shift(back[-1][2:], "z", -1)
    spread = from_everyone(got, "z")
    cols = [spread, shift(spread, "y", 1), shift(spread, "y", 2), shift(spread, "y", -1)]
    return forth + back[1:] + [far_a, far_b] + cols


def plan_first(idx):
    half, y, z = idx[0], idx[1], idx[2]
    plan = []
    for d in range(4):
        for e in range(4):
            plan.append((d, e, half, (y + 4 - e) % 4, (z + 8 - d) % 8))
    for d in range(1, 4):
        for e in range(4):
            plan.append((3 + d, e, half, (y + 4 - e) % 4, (z + d) % 8))
    for e in range(2):
        plan.append((7, e, half, (y + 4 - e) % 4, (z + 4) % 8))
        plan.append((8, e, half, (y + 2 - e) % 4, (z + 4) % 8))
    for e in range(4):
        for q in range(8):
            plan.append((9 + e, q, 1 - half, (y + 4 - e) % 4, q))
    return plan


def gather_second(own, away):
    held = jnp.stack([own, shift(away, "xh", 1)])[None]
    for bit in (1, 2, 4):
        held = jnp.concatenate([held, flip(held, "z", bit)])
    return [held, shift(held, "y", 1), shift(held, "y", 2), shift(held, "y", -1)]


def plan_second(idx):
    half, y, z = idx[0], idx[1], idx[2]
    plan = []
    for e in range(4):
        for q in range(8):
            for h in range(2):
                plan.append((e, (q, h), half if h == 0 else 1 - half, (y + 4 - e) % 4, z ^ q))
    return plan


def fetch_weights(plan, pieces, first, count, dst, sem):
    for piece, at, half, y, z in plan:
        at = at if isinstance(at, tuple) else (at,)
        src = pieces[piece].at[at + (pl.ds(first, count),)]
        pltpu.make_async_copy(src, dst.at[:, half, y, z], sem).start()


def wait_all(dst, sem):
    pltpu.make_async_copy(dst, dst, sem).wait()


def in_kernel(plan_of, n_pieces, with_ends, *refs):
    idx, gain = refs[0], refs[1]
    pos = 2
    toks = refs[pos : pos + 8]
    pos += 8
    pieces = refs[pos : pos + n_pieces]
    pos += n_pieces
    if with_ends:
        ends_w = refs[pos]
        pos += 1
    gate, prod, last = refs[pos : pos + 3]
    pos += 3
    w_s, x_s, n_s, w_sem, x_sem = refs[pos:]
    chip = idx[0] * 2 + idx[3]
    co = idx[4]
    for r in range(4):
        owner = (chip + 4 - (0, 1, 3, 2)[r]) % 4
        xh, xl = owner // 2, owner % 2
        for c in range(2):
            core = co if c == 0 else 1 - co
            col = pl.multiple_of((xl * 2 + core) * 512, 512)
            pltpu.make_async_copy(toks[c * 4 + r], x_s.at[xh, :, pl.ds(col, 512)], x_sem).start()
    fetch_weights(plan_of(idx), pieces, 0, 3, w_s, w_sem)
    wait_all(x_s, x_sem)
    g = gain[...]
    step = 32

    def norm(i, carry):
        for h in range(2):
            rows = pl.ds(pl.multiple_of(i * step, step), step)
            x = x_s[h, rows, :].astype(F32)
            factor = lax.rsqrt(jnp.mean(x * x, axis=1, keepdims=True) + 1e-06)
            n_s[h, rows, :] = (x * factor * g).astype(BF)
        return carry

    lax.fori_loop(0, 256 // step, norm, 0)
    wait_all(w_s, w_sem)
    for h in range(2):
        n = n_s[h]
        a = jnp.dot(n, w_s[0].reshape(2048, 256), preferred_element_type=F32)
        b = jnp.dot(n, w_s[2].reshape(2048, 256), preferred_element_type=F32)
        p = (a * b).astype(BF)
        prod[h] = p
        gate[h] = jnp.dot(n, w_s[1].reshape(2048, 256), preferred_element_type=F32)
        if with_ends:
            e = jnp.dot(ends_w[...], p, preferred_element_type=F32)
            e = own_group(e.reshape(16, 16, 256)).astype(BF)
            for k in range(8):
                last[k, h] = e
        else:
            last[h] = p[128:, :]


def own_group(v):
    lane = lax.broadcasted_iota(jnp.int32, v.shape[1:], 1) // GROUP
    out = jnp.where(lane == 0, v[0], 0.0)
    for k in range(1, v.shape[0]):
        out = jnp.where(lane == k, v[k], out)
    return out


def project_in(idx, gain, toks, pieces, plan_of, ends_w):
    with_ends = ends_w is not None
    last = (8, 2, 16, 256) if with_ends else (2, 128, 256)
    args = [idx, gain.reshape(1, -1), *toks, *pieces] + ([ends_w] if with_ends else [])
    specs = [SM, VM] + [ANY] * (len(toks) + len(pieces)) + ([VM] if with_ends else [])
    return pl.pallas_call(
        functools.partial(in_kernel, plan_of, len(pieces), with_ends),
        out_shape=(
            jax.ShapeDtypeStruct((2, 256, 256), F32),
            jax.ShapeDtypeStruct((2, 256, 256), BF),
            jax.ShapeDtypeStruct(last, BF),
        ),
        in_specs=specs,
        out_specs=(VM, VM, VM),
        scratch_shapes=[
            pltpu.VMEM((3, 2, 4, 8, 32, 256), BF),
            pltpu.VMEM((2, 256, 2048), BF),
            pltpu.VMEM((2, 256, 2048), BF),
            pltpu.SemaphoreType.DMA,
            pltpu.SemaphoreType.DMA,
        ],
        cost_estimate=pl.CostEstimate(flops=2 * 512 * 2048 * 768, bytes_accessed=7 << 20, transcendentals=0),
    )(*args)


def out_sums(gated, w_s, idx, away, keep, mine, theirs):
    half, co = idx[0], idx[4]
    for xl in range(2):
        for ref, core in ((away, 1 - co), (keep, co)):
            tp = xl * 2 + core
            w = w_s[0, tp // 2, pl.ds((tp % 2) * 2, 2)].reshape(512, 256)
            for h in range(2):
                r = lax.dot_general(gated[h], w, (((1,), (1,)), ((), ())), preferred_element_type=F32)
                ref[h, xl] = r.astype(ref.dtype)
    first = half == 0
    mine[...] = jnp.where(first, gated[0], gated[1]).T
    theirs[...] = jnp.where(first, gated[1], gated[0]).T


def medium_kernel(plan_of, n_pieces, *refs):
    idx, gate, prod, rim, rows = refs[:5]
    pieces = refs[5 : 5 + n_pieces]
    away, keep, mine, theirs, w_s, sem = refs[5 + n_pieces :]
    fetch_weights(plan_of(idx), pieces, 3, 1, w_s, sem)
    first = idx[1] * 8 + idx[2] == 0
    t = rows[...].reshape(16 * TAPS, 2 * TAPS)
    gated = []
    for h in range(2):
        if h == 0:
            prior = jnp.where(first, jnp.zeros_like(rim[0]), rim[0])
        else:
            prior = jnp.where(first, rim[0], rim[1])
        halves = []
        for j in range(2):
            window = jnp.concatenate([prior, prod[h, :TAPS]], axis=0) if j == 0 else prod[h]
            full = jnp.dot(t, window, preferred_element_type=F32)
            halves.append(own_group(full.reshape(16, TAPS, 256)))
        medium = jnp.concatenate(halves, axis=0)
        gated.append((gate[h] * medium).astype(BF))
    wait_all(w_s, sem)
    out_sums(gated, w_s, idx, away, keep, mine, theirs)


OUT_SHAPES = (
    jax.ShapeDtypeStruct((2, 2, 256, 512), BF),
    jax.ShapeDtypeStruct((2, 2, 256, 512), F32),
    jax.ShapeDtypeStruct((256, 256), BF),
    jax.ShapeDtypeStruct((256, 256), BF),
)
OUT_SCRATCH = [pltpu.VMEM((1, 2, 4, 8, 32, 256), BF), pltpu.SemaphoreType.DMA]


def medium_out(idx, gate, prod, rim, rows, pieces, plan_of):
    return pl.pallas_call(
        functools.partial(medium_kernel, plan_of, len(pieces)),
        out_shape=OUT_SHAPES,
        in_specs=[SM, VM, VM, VM, VM] + [ANY] * len(pieces),
        out_specs=(VM,) * 4,
        scratch_shapes=OUT_SCRATCH,
        cost_estimate=pl.CostEstimate(flops=2 * 512 * 2048 * 768, bytes_accessed=7 << 20, transcendentals=0),
    )(idx, gate, prod, rim, rows, *pieces)


def within_kernel(rows, prod, out):
    for h in range(2):
        full = jnp.dot(rows[...].reshape(16 * 256, 256), prod[h], preferred_element_type=F32)
        out[h] = own_group(full.reshape(16, 256, 256))


def within_block(rows, prod):
    return pl.pallas_call(
        within_kernel,
        out_shape=jax.ShapeDtypeStruct((2, 256, 256), F32),
        in_specs=[VM, VM],
        out_specs=VM,
        cost_estimate=pl.CostEstimate(flops=2 * 8192 * 256 * 256, bytes_accessed=3 << 20, transcendentals=0),
    )(rows, prod)


def combined(idx_here, count, span, rate, pieces):
    before, total = 0.0, 0.0
    for q in range(count):
        v = pieces[q].astype(F32)
        gap = (idx_here - 1 - q).astype(F32)
        w = jnp.where(gap >= 0, jnp.exp(-rate * (span * jnp.maximum(gap, 0.0))), 0.0)
        before = before + w * v
        total = total + jnp.exp(-rate * (span * float(count - 1 - q))) * v
    return before, total


def row_kernel(idx, rate, ends, before, total):
    b, t = combined(idx[2], 8, 256.0, rate[...], ends)
    before[...] = b
    for k in range(4):
        total[k] = t.astype(BF)


def row_states(idx, rate, ends):
    return pl.pallas_call(
        row_kernel,
        out_shape=(jax.ShapeDtypeStruct((2, 16, 256), F32), jax.ShapeDtypeStruct((4, 2, 16, 256), BF)),
        in_specs=[SM, VM, VM],
        out_specs=(VM, VM),
    )(idx, rate, ends)


def long_kernel(plan_of, n_pieces, *refs):
    idx, gate, within, rate, before, totals, starts = refs[:7]
    pieces = refs[7 : 7 + n_pieces]
    away, keep, mine, theirs, w_s, sem = refs[7 + n_pieces :]
    fetch_weights(plan_of(idx), pieces, 3, 1, w_s, sem)
    r = rate[...]
    y, z = idx[1].astype(F32), idx[2].astype(F32)
    b, t = combined(idx[1], 4, 2048.0, r, totals)
    carry = jnp.exp(-r * (2048.0 * y))
    decay = jnp.exp(-r * (256.0 * z))
    entering = [before[0] + decay * b[0], before[1] + decay * (b[1] + carry * t[0])]
    lane = lax.broadcasted_iota(jnp.int32, (16, 256), 1) // GROUP
    gated = []
    for h in range(2):
        spread = jnp.concatenate([jnp.where(lane == k, entering[h], 0.0) for k in range(16)], axis=0)
        carried = jnp.dot(starts[...], spread.astype(BF), preferred_element_type=F32)
        gated.append((gate[h] * (within[h] + carried)).astype(BF))
    wait_all(w_s, sem)
    out_sums(gated, w_s, idx, away, keep, mine, theirs)


def long_out(idx, gate, within, rate, before, totals, starts, pieces, plan_of):
    return pl.pallas_call(
        functools.partial(long_kernel, plan_of, len(pieces)),
        out_shape=OUT_SHAPES,
        in_specs=[SM] + [VM] * 6 + [ANY] * len(pieces),
        out_specs=(VM,) * 4,
        scratch_shapes=OUT_SCRATCH,
        cost_estimate=pl.CostEstimate(flops=2 * 512 * 2048 * 256, bytes_accessed=7 << 20, transcendentals=0),
    )(idx, gate, within, rate, before, totals, starts, *pieces)


def slide_kernel(taps, lags, medium, local):
    for k in range(16):
        wide = jnp.broadcast_to(taps[k : k + 1, :], (TAPS, 256))
        medium[k] = pltpu.roll(wide, 0, 1, stride=1, stride_axis=0).astype(BF)
        wide = jnp.broadcast_to(lags[k : k + 1, :], (256, 256))
        turned = pltpu.roll(wide, 0, 1, stride=1, stride_axis=0)
        row = lax.broadcasted_iota(jnp.int32, (256, 256), 0)
        col = lax.broadcasted_iota(jnp.int32, (256, 256), 1)
        local[k] = jnp.where(col <= row, turned, 0.0).astype(BF)


def slide_filters(taps, lags):
    return pl.pallas_call(
        slide_kernel,
        out_shape=(jax.ShapeDtypeStruct((16, TAPS, 256), BF), jax.ShapeDtypeStruct((16, 256, 256), BF)),
        in_specs=[VM, VM],
        out_specs=(VM, VM),
    )(taps, lags)


def gather_tokens(block):
    here = [block, ring_shift(block, 1), ring_shift(block, -1), ring_shift(block, 2)]
    return here + [flip(v, "co", 1) for v in here]


def reduced(away, keep):
    got = flip(away, "co", 1)
    summed = (keep + got.astype(F32)).astype(BF).reshape(4, 256, 512)
    return jnp.sum(lax.all_to_all(summed, RING, 0, 0, tiled=True).astype(F32), axis=0)


def placed(mine, theirs, half):
    got = shift(theirs, "xh", 1)
    return jnp.concatenate([jnp.where(half == 0, mine, got), jnp.where(half == 0, got, mine)], axis=0)


def filters_of(mr_filter, li_rate, li_residue, half):
    def part(v):
        n = v.shape[0] // 2
        return lax.dynamic_slice_in_dim(v, half * n, n, 0)

    mr, rate, residue = part(mr_filter).astype(F32), part(li_rate), part(li_residue)
    zeros = jnp.zeros((16, TAPS), F32)
    taps = jnp.concatenate([zeros[:, :1], mr[:, ::-1], zeros[:, 1:]], axis=1)
    weight = residue * jnp.sqrt(2.0 * rate)
    lag = jnp.asarray([0.0] + [256.0 - s for s in range(1, 256)], F32)
    lags = jnp.sum(weight[:, :, None] * jnp.exp(-rate[:, :, None] * lag), axis=1)
    medium_rows, local_rows = slide_filters(taps, lags)
    offs = jnp.arange(256, dtype=F32)
    flat = rate.reshape(256)
    ends_w = jnp.exp(-flat[:, None] * (255.0 - offs)).astype(BF)
    starts = (weight.reshape(256) * jnp.exp(-flat * (offs[:, None] + 1.0))).astype(BF)
    rate_mc = jnp.repeat(rate.T, GROUP, axis=1)
    return medium_rows, local_rows, ends_w, starts, rate_mc


def per_device(hidden, gain_a, in_a, mr_filter, out_a, gain_b, in_b, li_rate, li_residue, out_b):
    half = lax.axis_index("xh")
    idx = jnp.stack([lax.axis_index(a) for a in ("xh", "y", "z", "xl", "co")]).astype(jnp.int32)
    pieces_a = gather_first(*column_halves(in_a, out_a, half))
    toks = gather_tokens(hidden)
    medium_rows, local_rows, ends_w, starts, rate_mc = filters_of(mr_filter, li_rate, li_residue, half)
    pieces_b = gather_second(*column_halves(in_b, out_b, half))

    gate, prod, tail = project_in(idx, gain_a, toks, pieces_a, plan_first, None)
    rim = lax.ppermute(tail, ROWS, [(i, (i + 1) % 32) for i in range(32)])
    away, keep, mine, theirs = medium_out(idx, gate, prod, rim, medium_rows, pieces_a, plan_first)
    after_a = (hidden.astype(F32) + reduced(away, keep)).astype(BF)
    gated_medium = placed(mine, theirs, half)

    toks = gather_tokens(after_a)
    gate, prod, ends = project_in(idx, gain_b, toks, pieces_b, plan_second, ends_w)
    by_z = lax.all_to_all(ends, "z", 0, 0, tiled=True)
    within = within_block(local_rows, prod)
    before, total = row_states(idx, rate_mc, by_z)
    by_y = lax.all_to_all(total, "y", 0, 0, tiled=True)
    away, keep, mine, theirs = long_out(idx, gate, within, rate_mc, before, by_y, starts, pieces_b, plan_second)
    mixed = (after_a.astype(F32) + reduced(away, keep)).astype(BF)
    gated_long = placed(mine, theirs, half)
    return mixed, gated_medium, gated_long


def solution(mesh):
    split = Mesh(mesh.devices.reshape(2, 4, 8, 2, 2), ("xh", "y", "z", "xl", "co"))
    in_specs = (
        P(CTX, TP),
        P(),
        P(None, CTX, TP),
        P(TP, None),
        P(TP, CTX),
        P(),
        P(None, CTX, TP),
        P(TP, None),
        P(TP, None),
        P(TP, CTX),
    )
    out_specs = (P(CTX, TP), P(TP, CTX), P(TP, CTX))
    return jax.shard_map(per_device, mesh=split, in_specs=in_specs, out_specs=out_specs, check_vma=False)
```

```python
import jax
import jax.numpy as jnp
from jax import lax
from jax.experimental import pallas as pl
from jax.experimental.pallas import tpu as pltpu
from jax.sharding import Mesh
from jax.sharding import PartitionSpec as P


GROUP = 16
TAPS = 128
CTX = ("xh", "y", "z")
TP = ("xl", "co")
RING = ("xh", "xl")
ROWS = ("y", "z")
BF = jnp.bfloat16
F32 = jnp.float32
SIZES = {"xh": 2, "y": 4, "z": 8, "xl": 2, "co": 2}


ANY = pl.BlockSpec(memory_space=pl.ANY)
VM = pl.BlockSpec(memory_space=pltpu.VMEM)
SM = pl.BlockSpec(memory_space=pltpu.SMEM)


def shift(value, axis, steps):
    n = SIZES[axis]
    return lax.ppermute(value, axis, [(i, (i + steps) % n) for i in range(n)])


def flip(value, axis, bit):
    return lax.ppermute(value, axis, [(i, i ^ bit) for i in range(SIZES[axis])])


def ring_shift(value, steps):
    return lax.ppermute(value, RING, [(i, (i + steps) % 4) for i in range(4)])


def exchange(blocks, axis):
    return lax.all_to_all(blocks, axis, split_axis=0, concat_axis=0, tiled=True)


def column_halves(in_w, out_w, half):
    both = jnp.concatenate([in_w, out_w.T[None]], axis=0)
    _, _, cols = both.shape
    own = lax.dynamic_slice_in_dim(both, half * (cols // 2), cols // 2, 2)
    away = lax.dynamic_slice_in_dim(both, (1 - half) * (cols // 2), cols // 2, 2)
    return own, away


def gather_first(own, away):
    spread = exchange(jnp.broadcast_to(own, (8, *own.shape)), "z")
    got = shift(away, "xh", 1)
    ys = [got, shift(got, "y", 1), shift(got, "y", 2), shift(got, "y", -1)]
    bundle = jnp.stack(ys)
    forth, back = [bundle], [bundle]
    for _ in range(1, 4):
        forth.append(shift(forth[-1], "z", 1))
        back.append(shift(back[-1], "z", -1))
    far_a = shift(forth[-1][:2], "z", 1)
    far_b = shift(back[-1][2:], "z", -1)
    cols = [spread] + [shift(spread, "y", d) for d in (1, 2, -1)]
    return forth + back[1:] + [far_a, far_b] + cols


def fetch_first(idx, pieces, first, count, dst, sem):
    half, y, z = idx[0], idx[1], idx[2]
    kinds = pl.ds(first, count)

    def send(piece, at, h, yy, zz):
        pltpu.make_async_copy(pieces[piece].at[at, kinds], dst.at[:, h, yy, zz], sem).start()

    def near(e, carry):
        yy = (y + 4 - e) % 4
        for piece, back in ((0, 8), (1, 7), (2, 6), (3, 5), (4, 9), (5, 10), (6, 11)):
            send(piece, e, 1 - half, yy, (z + back) % 8)
        return carry

    def far(e, carry):
        send(7, e, 1 - half, (y + 4 - e) % 4, (z + 4) % 8)
        send(8, e, 1 - half, (y + 2 - e) % 4, (z + 4) % 8)
        return carry

    def column(q, carry):
        for e in range(4):
            send(9 + e, q, half, (y + 4 - e) % 4, q)
        return carry

    lax.fori_loop(0, 4, near, 0)
    lax.fori_loop(0, 2, far, 0)
    lax.fori_loop(0, 8, column, 0)


def gather_second(own, away):
    held = jnp.stack([own, shift(away, "xh", 1)], axis=1)[:, None]
    for bit in (4, 2, 1):
        held = jnp.concatenate([held, flip(held, "z", bit)], axis=1)
    ins = [held] + [shift(held[:3], "y", d) for d in (1, 2, -1)]
    outs = [held] + [shift(held[3:], "y", d) for d in (1, 2, -1)]
    return ins, outs


def fetch_second(idx, pieces, first, count, dst, sem):
    half, y, z = idx[0], idx[1], idx[2]

    def column(q, carry):
        zz = z ^ ((q % 2) * 4 + (q // 2 % 2) * 2 + q // 4)
        for e in range(4):
            start = first if pieces[e].shape[0] == 4 else 0
            for h in range(2):
                src = pieces[e].at[pl.ds(start, count), q, h]
                yy = (y + 4 - e) % 4
                pltpu.make_async_copy(src, dst.at[:, half if h == 0 else 1 - half, yy, zz], sem).start()
        return carry

    lax.fori_loop(0, 8, column, 0)


def wait_all(dst, sem):
    pltpu.make_async_copy(dst, dst, sem).wait()


def place_tokens(idx, toks, x_s, x_sem):
    chip = idx[0] * 2 + idx[3]
    co = idx[4]
    for r in range(4):
        owner = (chip + 4 - (0, 1, 3, 2)[r]) % 4
        xh, xl = owner // 2, owner % 2
        for c in range(2):
            core = co if c == 0 else 1 - co
            col = pl.multiple_of((xl * 2 + core) * 512, 512)
            pltpu.make_async_copy(toks[c * 4 + r], x_s.at[xh, :, pl.ds(col, 512)], x_sem).start()


def normalize(x_s, gain, n_s):
    g = gain[...]
    step = 32

    def norm(i, carry):
        for h in range(2):
            rows = pl.ds(pl.multiple_of(i * step, step), step)
            x = x_s[h, rows, :].astype(F32)
            factor = lax.rsqrt(jnp.mean(x * x, axis=1, keepdims=True) + 1e-06)
            n_s[h, rows, :] = (x * factor * g).astype(BF)
        return carry

    lax.fori_loop(0, 256 // step, norm, 0, unroll=2)


def norm_kernel(idx, gain, *refs):
    toks, n_o, x_s, x_sem = refs[:8], refs[8], refs[9], refs[10]
    place_tokens(idx, toks, x_s, x_sem)
    wait_all(x_s, x_sem)
    normalize(x_s, gain, n_o)


def norm_rows(idx, gain, toks):
    return pl.pallas_call(
        norm_kernel,
        out_shape=jax.ShapeDtypeStruct((2, 256, 2048), BF),
        in_specs=[SM, VM] + [ANY] * 8,
        out_specs=VM,
        scratch_shapes=[pltpu.VMEM((2, 256, 2048), BF), pltpu.SemaphoreType.DMA],
        cost_estimate=pl.CostEstimate(flops=8 << 20, bytes_accessed=4 << 20, transcendentals=0),
    )(idx, gain.reshape(1, -1), *toks)


def products(n_s, w_s, gate, prod):
    def half(h, carry):
        n = n_s[h]
        a = jnp.dot(n, w_s[0].reshape(2048, 256), preferred_element_type=F32)
        b = jnp.dot(n, w_s[2].reshape(2048, 256), preferred_element_type=F32)
        prod[h] = (a * b).astype(BF)
        gate[h] = jnp.dot(n, w_s[1].reshape(2048, 256), preferred_element_type=F32)
        return carry

    lax.fori_loop(0, 2, half, 0)


def first_kernel(idx, n_s, *refs):
    pieces = refs[:-5]
    gate, prod, last, w_s, w_sem = refs[-5:]
    fetch_first(idx, pieces, 0, 3, w_s, w_sem)
    wait_all(w_s, w_sem)
    products(n_s, w_s, gate, prod)
    last[...] = prod[:, 128:, :]


IN_COST = pl.CostEstimate(flops=2 * 512 * 2048 * 768, bytes_accessed=7 << 20, transcendentals=0)


def first_in(idx, normed, pieces):
    return pl.pallas_call(
        first_kernel,
        out_shape=(
            jax.ShapeDtypeStruct((2, 256, 256), F32),
            jax.ShapeDtypeStruct((2, 256, 256), BF),
            jax.ShapeDtypeStruct((2, 128, 256), BF),
        ),
        in_specs=[SM, VM] + [ANY] * len(pieces),
        out_specs=(VM, VM, VM),
        scratch_shapes=[pltpu.VMEM((3, 2, 4, 8, 32, 256), BF), pltpu.SemaphoreType.DMA],
        cost_estimate=IN_COST,
    )(idx, normed, *pieces)


def second_kernel(idx, gain, ends_w, *refs):
    toks, pieces = refs[:8], refs[8:12]
    gate, prod, ends, w_s, x_s, n_s, w_sem, x_sem = refs[12:]
    place_tokens(idx, toks, x_s, x_sem)
    fetch_second(idx, pieces, 0, 3, w_s, w_sem)
    wait_all(x_s, x_sem)
    normalize(x_s, gain, n_s)
    wait_all(w_s, w_sem)
    products(n_s, w_s, gate, prod)
    for h in range(2):
        e = jnp.dot(ends_w[...], prod[h], preferred_element_type=F32)
        e = own_group(e.reshape(16, 16, 256)).astype(BF)
        for k in range(8):
            ends[k, h] = e


def second_in(idx, gain, ends_w, toks, pieces):
    return pl.pallas_call(
        second_kernel,
        out_shape=(
            jax.ShapeDtypeStruct((2, 256, 256), F32),
            jax.ShapeDtypeStruct((2, 256, 256), BF),
            jax.ShapeDtypeStruct((8, 2, 16, 256), BF),
        ),
        in_specs=[SM, VM, VM] + [ANY] * 12,
        out_specs=(VM, VM, VM),
        scratch_shapes=[
            pltpu.VMEM((3, 2, 4, 8, 32, 256), BF),
            pltpu.VMEM((2, 256, 2048), BF),
            pltpu.VMEM((2, 256, 2048), BF),
            pltpu.SemaphoreType.DMA,
            pltpu.SemaphoreType.DMA,
        ],
        cost_estimate=IN_COST,
    )(idx, gain.reshape(1, -1), ends_w, *toks, *pieces)


def own_group(v):
    lane = lax.broadcasted_iota(jnp.int32, v.shape[1:], 1) // GROUP
    out = jnp.where(lane == 0, v[0], 0.0)
    for k in range(1, v.shape[0]):
        out = jnp.where(lane == k, v[k], out)
    return out


def split_out(w_s, idx, keep, send):
    for ref, core in ((keep, idx[4]), (send, 1 - idx[4])):
        for xl in range(2):
            tp = xl * 2 + core
            ref[xl] = w_s[0, tp // 2, pl.ds((tp % 2) * 2, 2)].reshape(512, 256)


SPLIT = (jax.ShapeDtypeStruct((2, 512, 256), BF),) * 2
OUT_PLACE = [pltpu.VMEM((1, 2, 4, 8, 32, 256), BF), pltpu.SemaphoreType.DMA]
SQUARE = jax.ShapeDtypeStruct((256, 256), BF)
GATED = jax.ShapeDtypeStruct((2, 256, 256), BF)


def out_kernel(here, there, w_here, w_there, out):
    dims = (((1,), (1,)), ((), ()))

    def part(i, carry):
        h, xl = i // 2, i % 2
        a = lax.dot_general(here[h], w_here[xl], dims, preferred_element_type=F32)
        b = lax.dot_general(there[h], w_there[xl], dims, preferred_element_type=F32)
        out[i] = (a + b).astype(BF)
        return carry

    lax.fori_loop(0, 4, part, 0)


def out_sums(here, there, w_here, w_there):
    return pl.pallas_call(
        out_kernel,
        out_shape=jax.ShapeDtypeStruct((4, 256, 512), BF),
        in_specs=[VM] * 4,
        out_specs=VM,
        cost_estimate=pl.CostEstimate(flops=2 * 512 * 512 * 1024, bytes_accessed=3 << 20, transcendentals=0),
    )(here, there, w_here, w_there)


def medium_kernel(idx, gate, prod, rim, rows, gated, ext):
    first = idx[1] * 8 + idx[2] == 0
    ext[0, :TAPS, :] = jnp.where(first, jnp.zeros_like(rim[0]), rim[0])
    ext[1, :TAPS, :] = jnp.where(first, rim[0], rim[1])
    ext[:, TAPS:, :] = prod[...]

    def block(i, carry):
        h = i // 2
        at = pl.multiple_of((i % 2) * TAPS, TAPS)
        window = ext[h, pl.ds(at, 2 * TAPS), :]
        full = jnp.dot(rows[...].reshape(16 * TAPS, 2 * TAPS), window, preferred_element_type=F32)
        medium = own_group(full.reshape(16, TAPS, 256))
        gated[h, pl.ds(at, TAPS), :] = (gate[h, pl.ds(at, TAPS), :] * medium).astype(BF)
        return carry

    lax.fori_loop(0, 4, block, 0)


def medium_gated(idx, gate, prod, rim, rows):
    return pl.pallas_call(
        medium_kernel,
        out_shape=GATED,
        in_specs=[SM, VM, VM, VM, VM],
        out_specs=VM,
        scratch_shapes=[pltpu.VMEM((2, 384, 256), BF)],
        cost_estimate=pl.CostEstimate(flops=2 * 8192 * 256 * 256, bytes_accessed=3 << 20, transcendentals=0),
    )(idx, gate, prod, rim, rows)


def within_kernel(idx, rows, prod, gated, *refs):
    pieces = refs[:4]
    out, mine, theirs, keep, send, w_s, sem = refs[4:]
    fetch_second(idx, pieces, 3, 1, w_s, sem)
    mine[...] = gated[idx[0]].T
    theirs[...] = gated[1 - idx[0]].T

    def half(h, carry):
        full = jnp.dot(rows[...].reshape(16 * 256, 256), prod[h], preferred_element_type=F32)
        out[h] = own_group(full.reshape(16, 256, 256))
        return carry

    lax.fori_loop(0, 2, half, 0)
    wait_all(w_s, sem)
    split_out(w_s, idx, keep, send)


def within_block(idx, rows, prod, gated, pieces):
    return pl.pallas_call(
        within_kernel,
        out_shape=(jax.ShapeDtypeStruct((2, 256, 256), F32), SQUARE, SQUARE, *SPLIT),
        in_specs=[SM, VM, VM, VM] + [ANY] * 4,
        out_specs=(VM,) * 5,
        scratch_shapes=OUT_PLACE,
        cost_estimate=pl.CostEstimate(flops=2 * 8192 * 256 * 256, bytes_accessed=5 << 20, transcendentals=0),
    )(idx, rows, prod, gated, *pieces)


def combined(idx_here, count, span, rate, pieces):
    before, total = 0.0, 0.0
    for q in range(count):
        v = pieces[q].astype(F32)
        gap = (idx_here - 1 - q).astype(F32)
        w = jnp.where(gap >= 0, jnp.exp(-rate * (span * jnp.maximum(gap, 0.0))), 0.0)
        before = before + w * v
        total = total + jnp.exp(-rate * (span * float(count - 1 - q))) * v
    return before, total


def row_kernel(idx, rate, ends, before, total):
    b, t = combined(idx[2], 8, 256.0, rate[...], ends)
    before[...] = b
    for k in range(4):
        total[k] = t.astype(BF)


def row_states(idx, rate, ends):
    return pl.pallas_call(
        row_kernel,
        out_shape=(jax.ShapeDtypeStruct((2, 16, 256), F32), jax.ShapeDtypeStruct((4, 2, 16, 256), BF)),
        in_specs=[SM, VM, VM],
        out_specs=(VM, VM),
    )(idx, rate, ends)


def long_kernel(idx, gate, within, rate, before, totals, starts, gated, mine, theirs):
    r = rate[...]
    y, z = idx[1].astype(F32), idx[2].astype(F32)
    b, t = combined(idx[1], 4, 2048.0, r, totals)
    carry = jnp.exp(-r * (2048.0 * y))
    decay = jnp.exp(-r * (256.0 * z))
    entering = [before[0] + decay * b[0], before[1] + decay * (b[1] + carry * t[0])]
    lane = lax.broadcasted_iota(jnp.int32, (16, 256), 1) // GROUP
    for h in range(2):
        spread = jnp.concatenate([jnp.where(lane == k, entering[h], 0.0) for k in range(16)], axis=0)
        carried = jnp.dot(starts[...], spread.astype(BF), preferred_element_type=F32)
        gated[h] = (gate[h] * (within[h] + carried)).astype(BF)
    mine[...] = gated[idx[0]].T
    theirs[...] = gated[1 - idx[0]].T


def long_gated(idx, gate, within, rate, before, totals, starts):
    return pl.pallas_call(
        long_kernel,
        out_shape=(GATED, SQUARE, SQUARE),
        in_specs=[SM] + [VM] * 6,
        out_specs=(VM,) * 3,
        cost_estimate=pl.CostEstimate(flops=2 * 512 * 256 * 256, bytes_accessed=2 << 20, transcendentals=0),
    )(idx, gate, within, rate, before, totals, starts)


def slide_kernel(idx, taps, lags, *refs):
    pieces = refs[:13]
    medium, local, keep, send, w_s, sem = refs[13:]
    fetch_first(idx, pieces, 3, 1, w_s, sem)
    row = lax.broadcasted_iota(jnp.int32, (256, 256), 0)
    col = lax.broadcasted_iota(jnp.int32, (256, 256), 1)

    def group(k, carry):
        wide = jnp.broadcast_to(taps[pl.ds(k, 1), :], (TAPS, 256))
        medium[k] = pltpu.roll(wide, 0, 1, stride=1, stride_axis=0).astype(BF)
        wide = jnp.broadcast_to(lags[pl.ds(k, 1), :], (256, 256))
        turned = pltpu.roll(wide, 0, 1, stride=1, stride_axis=0)
        local[k] = jnp.where(col <= row, turned, 0.0).astype(BF)
        return carry

    lax.fori_loop(0, 16, group, 0)
    wait_all(w_s, sem)
    split_out(w_s, idx, keep, send)


def slide_filters(idx, taps, lags, pieces):
    return pl.pallas_call(
        slide_kernel,
        out_shape=(
            jax.ShapeDtypeStruct((16, TAPS, 256), BF),
            jax.ShapeDtypeStruct((16, 256, 256), BF),
            *SPLIT,
        ),
        in_specs=[SM, VM, VM] + [ANY] * len(pieces),
        out_specs=(VM,) * 4,
        scratch_shapes=OUT_PLACE,
    )(idx, taps, lags, *pieces)


def gather_tokens(block):
    here = [block] + [ring_shift(block, d) for d in (1, -1, 2)]
    return here + [flip(v, "co", 1) for v in here]


def reduced(before, here, w_here, w_there):
    there = flip(here, "co", 1)
    summed = out_sums(here, there, w_here, w_there)
    parts = exchange(summed, RING).astype(F32)
    return (before.astype(F32) + ((parts[0] + parts[1]) + (parts[2] + parts[3]))).astype(BF)


def placed(mine, theirs, half):
    got = shift(theirs, "xh", 1)
    return jnp.concatenate([jnp.where(half == 0, mine, got), jnp.where(half == 0, got, mine)], axis=0)


def filters_of(mr_filter, li_rate, li_residue, half):
    def part(v):
        n = v.shape[0] // 2
        return lax.dynamic_slice_in_dim(v, half * n, n, 0)

    mr, rate, residue = part(mr_filter).astype(F32), part(li_rate), part(li_residue)
    zeros = jnp.zeros((16, TAPS), F32)
    taps = jnp.concatenate([zeros[:, :1], mr[:, ::-1], zeros[:, 1:]], axis=1)
    weight = residue * jnp.sqrt(2.0 * rate)
    lag = jnp.asarray([0.0] + [256.0 - s for s in range(1, 256)], F32)
    lags = jnp.sum(weight[:, :, None] * jnp.exp(-rate[:, :, None] * lag), axis=1)
    offs = jnp.arange(256, dtype=F32)
    flat = rate.reshape(256)
    ends_w = jnp.exp(-flat[:, None] * (255.0 - offs)).astype(BF)
    starts = (weight.reshape(256) * jnp.exp(-flat * (offs[:, None] + 1.0))).astype(BF)
    rate_mc = jnp.repeat(rate.T, GROUP, axis=1)
    return taps, lags, ends_w, starts, rate_mc


def both_operators(hidden, gain_a, in_a, mr_filter, out_a, gain_b, in_b, li_rate, li_residue, out_b):
    half = lax.axis_index("xh")
    idx = jnp.stack([lax.axis_index(a) for a in ("xh", "y", "z", "xl", "co")]).astype(jnp.int32)
    pieces_a = gather_first(*column_halves(in_a, out_a, half))
    toks = gather_tokens(hidden)
    taps, lags, ends_w, starts, rate_mc = filters_of(mr_filter, li_rate, li_residue, half)
    ins_b, outs_b = gather_second(*column_halves(in_b, out_b, half))

    normed = norm_rows(idx, gain_a, toks)
    gate, prod, tail = first_in(idx, normed, pieces_a)
    rim = lax.ppermute(tail, ROWS, [(i, (i + 1) % 32) for i in range(32)])
    medium_rows, local_rows, w_here, w_away = slide_filters(idx, taps, lags, pieces_a)
    w_there = flip(w_away, "co", 1)
    gated_a = medium_gated(idx, gate, prod, rim, medium_rows)
    after_a = reduced(hidden, gated_a, w_here, w_there)

    toks = gather_tokens(after_a)
    gate, prod, ends = second_in(idx, gain_b, ends_w, toks, ins_b)
    by_z = exchange(ends, "z")
    within, mine, theirs, w_here, w_away = within_block(idx, local_rows, prod, gated_a, outs_b)
    w_there = flip(w_away, "co", 1)
    gated_medium = placed(mine, theirs, half)
    before, total = row_states(idx, rate_mc, by_z)
    by_y = exchange(total, "y")
    gated_b, mine, theirs = long_gated(idx, gate, within, rate_mc, before, by_y, starts)
    mixed = reduced(after_a, gated_b, w_here, w_there)
    gated_long = placed(mine, theirs, half)
    return mixed, gated_medium, gated_long


def solution(mesh):
    split = Mesh(mesh.devices.reshape(2, 4, 8, 2, 2), ("xh", "y", "z", "xl", "co"))
    in_specs = (
        P(CTX, TP),
        P(),
        P(None, CTX, TP),
        P(TP, None),
        P(TP, CTX),
        P(),
        P(None, CTX, TP),
        P(TP, None),
        P(TP, None),
        P(TP, CTX),
    )
    out_specs = (P(CTX, TP), P(TP, CTX), P(TP, CTX))
    return jax.shard_map(both_operators, mesh=split, in_specs=in_specs, out_specs=out_specs, check_vma=False)
```

```python
import jax
import jax.numpy as jnp
from jax import lax
from jax.experimental import pallas as pl
from jax.experimental.pallas import tpu as pltpu
from jax.sharding import Mesh
from jax.sharding import PartitionSpec as P


GROUP = 16
TAPS = 128
WINDOW = 256 + TAPS
CTX = ("xh", "y", "z")
TP = ("xl", "co")
RING = ("xh", "xl")
BF = jnp.bfloat16
F32 = jnp.float32
SIZES = {"xh": 2, "y": 4, "z": 8, "xl": 2, "co": 2}


ANY = pl.BlockSpec(memory_space=pl.ANY)
VM = pl.BlockSpec(memory_space=pltpu.VMEM)
SM = pl.BlockSpec(memory_space=pltpu.SMEM)


def shift(value, axis, steps):
    n = SIZES[axis]
    return lax.ppermute(value, axis, [(i, (i + steps) % n) for i in range(n)])


def flip(value, axis, bit):
    return lax.ppermute(value, axis, [(i, i ^ bit) for i in range(SIZES[axis])])


def ring_shift(value, steps):
    return lax.ppermute(value, RING, [(i, (i + steps) % 4) for i in range(4)])


def exchange(blocks, axis):
    return lax.all_to_all(blocks, axis, split_axis=0, concat_axis=0, tiled=True)


def column_halves(in_w, out_w, half):
    both = jnp.concatenate([in_w, out_w.T[None]], axis=0)
    _, _, cols = both.shape
    own = lax.dynamic_slice_in_dim(both, half * (cols // 2), cols // 2, 2)
    away = lax.dynamic_slice_in_dim(both, (1 - half) * (cols // 2), cols // 2, 2)
    return own, away


def gather_first(own, away):
    spread = exchange(jnp.broadcast_to(own, (8, *own.shape)), "z")
    got = shift(away, "xh", 1)
    ys = [got, shift(got, "y", 1), shift(got, "y", 2), shift(got, "y", -1)]
    bundle = jnp.stack(ys)
    forth, back = [bundle], [bundle]
    for _ in range(1, 4):
        forth.append(shift(forth[-1], "z", 1))
        back.append(shift(back[-1], "z", -1))
    far = shift(forth[-1], "z", 1)
    cols = [spread] + [shift(spread, "y", d) for d in (1, 2, -1)]
    return forth + back[1:] + [far] + cols


def fetch_first(idx, pieces, first, count, dst, sem):
    half, y, z = idx[0], idx[1], idx[2]
    kinds = pl.ds(first, count)

    def send(piece, at, h, yy, zz):
        pltpu.make_async_copy(pieces[piece].at[at, kinds], dst.at[:, h, yy, zz], sem).start()

    def near(e, carry):
        yy = (y + 4 - e) % 4
        for piece, back in ((0, 8), (1, 7), (2, 6), (3, 5), (4, 9), (5, 10), (6, 11), (7, 12)):
            send(piece, e, 1 - half, yy, (z + back) % 8)
        return carry

    def column(q, carry):
        for e in range(4):
            send(8 + e, q, half, (y + 4 - e) % 4, q)
        return carry

    lax.fori_loop(0, 4, near, 0)
    lax.fori_loop(0, 8, column, 0)


def gather_second(own, away):
    both = jnp.stack([own, shift(away, "xh", 1)])
    held = exchange(jnp.broadcast_to(both, (8, *both.shape)), "z")
    part = held[:, :, :3]
    up, down = shift(part, "y", 1), shift(part, "y", -1)
    ins = [held, up, shift(up[:4], "y", 1), down, shift(down[4:], "y", -1)]
    outs = [held] + [shift(held[:, :, 3:], "y", d) for d in (1, 2, -1)]
    return ins, outs


def fetch_second(idx, pieces, first, count, dst, sem):
    half, y = idx[0], idx[1]

    def column(q, carry):
        for e in range(4):
            start = first if pieces[e].shape[2] == 4 else 0
            for k in range(2):
                low = pieces[e].shape[0] == 4
                ref, at = (pieces[e] if k == 0 else pieces[4], q) if low else (pieces[e], q + 4 * k)
                for h in range(2):
                    src = ref.at[at, h, pl.ds(start, count)]
                    place = dst.at[:, half if h == 0 else 1 - half, (y + 4 - e) % 4, q + 4 * k]
                    pltpu.make_async_copy(src, place, sem).start()
        return carry

    lax.fori_loop(0, 4, column, 0)


def wait_all(dst, sem):
    pltpu.make_async_copy(dst, dst, sem).wait()


def place_tokens(idx, toks, x_s, x_sem):
    chip = idx[0] * 2 + idx[3]
    for r, back in enumerate((0, 1, 3, 2)):
        owner = (chip + 4 - back) % 4
        xh, xl = owner // 2, owner % 2
        for c in range(2):
            core = idx[4] if c == 0 else 1 - idx[4]
            col = pl.multiple_of((xl * 2 + core) * 512, 512)
            pltpu.make_async_copy(toks[c * 4 + r], x_s.at[xh, :, pl.ds(col, 512)], x_sem).start()


def normalize(x_s, gain, n_s):
    g = gain[...]
    step = 32

    def norm(i, carry):
        for h in range(2):
            rows = pl.ds(pl.multiple_of(i * step, step), step)
            x = x_s[h, rows, :].astype(F32)
            factor = lax.rsqrt(jnp.mean(x * x, axis=1, keepdims=True) + 1e-06)
            n_s[h, rows, :] = (x * factor * g).astype(BF)
        return carry

    lax.fori_loop(0, x_s.shape[1] // step, norm, 0)


def norm_kernel(idx, gain, *refs):
    here, there = refs[:4], refs[4]
    n_o, x_s, x_sem = refs[5:]
    place_tokens(idx, list(here) + [there.at[k] for k in range(4)], x_s, x_sem)
    wait_all(x_s, x_sem)
    normalize(x_s, gain, n_o)


def norm_rows(idx, gain, toks):
    return pl.pallas_call(
        norm_kernel,
        out_shape=jax.ShapeDtypeStruct((2, WINDOW, 2048), BF),
        in_specs=[SM, VM] + [ANY] * 5,
        out_specs=VM,
        scratch_shapes=[pltpu.VMEM((2, WINDOW, 2048), BF), pltpu.SemaphoreType.DMA],
        cost_estimate=pl.CostEstimate(flops=8 << 20, bytes_accessed=4 << 20, transcendentals=0),
    )(idx, gain.reshape(1, -1), *toks)


def products(n_s, w_s, gate, prod):
    def half(h, carry):
        n = n_s[h]
        a = jnp.dot(n, w_s[0].reshape(2048, 256), preferred_element_type=F32)
        b = jnp.dot(n, w_s[2].reshape(2048, 256), preferred_element_type=F32)
        prod[h] = (a * b).astype(BF)
        gate[h] = jnp.dot(n, w_s[1].reshape(2048, 256), preferred_element_type=F32)
        return carry

    lax.fori_loop(0, 2, half, 0)


IN_COST = pl.CostEstimate(flops=2 * 512 * 2048 * 768, bytes_accessed=7 << 20, transcendentals=0)


def second_kernel(idx, gain, ends_w, *refs):
    here, (own, near, far), pieces = refs[:4], refs[4:7], refs[7:12]
    gate, prod, ends, w_s, x_s, n_s, w_sem, x_sem = refs[12:]
    place_tokens(idx, list(here) + [own, near.at[0], near.at[1], far], x_s, x_sem)
    fetch_second(idx, pieces, 0, 3, w_s, w_sem)
    wait_all(x_s, x_sem)
    normalize(x_s, gain, n_s)
    wait_all(w_s, w_sem)
    products(n_s, w_s, gate, prod)

    def states(h, carry):
        e = jnp.dot(ends_w[...], prod[h], preferred_element_type=F32)
        e = own_group(e.reshape(16, 16, 256)).astype(BF)
        for k in range(8):
            ends[k, h] = e
        return carry

    lax.fori_loop(0, 2, states, 0)


def second_in(idx, gain, ends_w, toks, pieces):
    return pl.pallas_call(
        second_kernel,
        out_shape=(
            jax.ShapeDtypeStruct((2, 256, 256), F32),
            jax.ShapeDtypeStruct((2, 256, 256), BF),
            jax.ShapeDtypeStruct((8, 2, 16, 256), BF),
        ),
        in_specs=[SM, VM, VM] + [ANY] * 12,
        out_specs=(VM, VM, VM),
        scratch_shapes=[
            pltpu.VMEM((3, 2, 4, 8, 32, 256), BF),
            pltpu.VMEM((2, 256, 2048), BF),
            pltpu.VMEM((2, 256, 2048), BF),
            pltpu.SemaphoreType.DMA,
            pltpu.SemaphoreType.DMA,
        ],
        cost_estimate=IN_COST,
    )(idx, gain.reshape(1, -1), ends_w, *toks, *pieces)


def own_group(v):
    lane = lax.broadcasted_iota(jnp.int32, v.shape[1:], 1) // GROUP
    out = jnp.where(lane == 0, v[0], 0.0)
    for k in range(1, v.shape[0]):
        out = jnp.where(lane == k, v[k], out)
    return out


def split_out(w_s, idx, keep, send):
    for ref, core in ((keep, idx[4]), (send, 1 - idx[4])):
        for xl in range(2):
            tp = xl * 2 + core
            ref[xl] = w_s[0, tp // 2, pl.ds((tp % 2) * 2, 2)].reshape(512, 256)


SPLIT = (jax.ShapeDtypeStruct((2, 512, 256), BF),) * 2
OUT_PLACE = [pltpu.VMEM((1, 2, 4, 8, 32, 256), BF), pltpu.SemaphoreType.DMA]
SQUARE = jax.ShapeDtypeStruct((256, 256), BF)
GATED = jax.ShapeDtypeStruct((2, 256, 256), BF)


def out_kernel(here, there, w_here, w_there, out):
    dims = (((1,), (1,)), ((), ()))
    g_here, g_there = here[...].reshape(512, 256), there[...].reshape(512, 256)

    def part(xl, carry):
        a = lax.dot_general(g_here, w_here[xl], dims, preferred_element_type=F32)
        b = lax.dot_general(g_there, w_there[xl], dims, preferred_element_type=F32)
        r = (a + b).astype(BF)
        out[xl] = r[:256]
        out[2 + xl] = r[256:]
        return carry

    lax.fori_loop(0, 2, part, 0)


def out_sums(here, there, w_here, w_there):
    return pl.pallas_call(
        out_kernel,
        out_shape=jax.ShapeDtypeStruct((4, 256, 512), BF),
        in_specs=[VM] * 4,
        out_specs=VM,
        cost_estimate=pl.CostEstimate(flops=2 * 512 * 512 * 1024, bytes_accessed=3 << 20, transcendentals=0),
    )(here, there, w_here, w_there)


def first_kernel(idx, n_s, rows, *refs):
    pieces = refs[:12]
    gated, keep, send, w_s, w_o, ext, gate, w_sem, o_sem = refs[12:]
    fetch_first(idx, pieces, 0, 3, w_s, w_sem)
    fetch_first(idx, pieces, 3, 1, w_o, o_sem)
    wait_all(w_s, w_sem)

    def half(h, carry):
        n = n_s[h]
        a = jnp.dot(n, w_s[0].reshape(2048, 256), preferred_element_type=F32)
        b = jnp.dot(n, w_s[2].reshape(2048, 256), preferred_element_type=F32)
        ext[h] = (a * b).astype(BF)
        gate[h] = jnp.dot(n_s[h, TAPS:, :], w_s[1].reshape(2048, 256), preferred_element_type=F32)
        return carry

    def block(i, carry):
        h = i // 2
        at = pl.multiple_of((i % 2) * TAPS, TAPS)
        window = ext[h, pl.ds(at, 2 * TAPS), :]
        full = jnp.dot(rows[...].reshape(16 * TAPS, 2 * TAPS), window, preferred_element_type=F32)
        medium = own_group(full.reshape(16, TAPS, 256))
        gated[h, pl.ds(at, TAPS), :] = (gate[h, pl.ds(at, TAPS), :] * medium).astype(BF)
        return carry

    lax.fori_loop(0, 2, half, 0)
    lax.fori_loop(0, 4, block, 0)
    wait_all(w_o, o_sem)
    split_out(w_o, idx, keep, send)


def first_gated(idx, normed, rows, pieces):
    return pl.pallas_call(
        first_kernel,
        out_shape=(GATED, *SPLIT),
        in_specs=[SM, VM, VM] + [ANY] * len(pieces),
        out_specs=(VM,) * 3,
        scratch_shapes=[
            pltpu.VMEM((3, 2, 4, 8, 32, 256), BF),
            pltpu.VMEM((1, 2, 4, 8, 32, 256), BF),
            pltpu.VMEM((2, WINDOW, 256), BF),
            pltpu.VMEM((2, 256, 256), F32),
            pltpu.SemaphoreType.DMA,
            pltpu.SemaphoreType.DMA,
        ],
        cost_estimate=pl.CostEstimate(flops=6 << 30, bytes_accessed=9 << 20, transcendentals=0),
    )(idx, normed, rows, *pieces)


def within_kernel(idx, rows, prod, gated, *refs):
    pieces = refs[:4]
    out, mine, theirs, keep, send, w_s, sem = refs[4:]
    fetch_second(idx, pieces, 3, 1, w_s, sem)
    mine[...] = gated[idx[0]].T
    theirs[...] = gated[1 - idx[0]].T

    def half(h, carry):
        full = jnp.dot(rows[...].reshape(16 * 256, 256), prod[h], preferred_element_type=F32)
        out[h] = own_group(full.reshape(16, 256, 256))
        return carry

    lax.fori_loop(0, 2, half, 0)
    wait_all(w_s, sem)
    split_out(w_s, idx, keep, send)


def within_block(idx, rows, prod, gated, pieces):
    return pl.pallas_call(
        within_kernel,
        out_shape=(jax.ShapeDtypeStruct((2, 256, 256), F32), SQUARE, SQUARE, *SPLIT),
        in_specs=[SM, VM, VM, VM] + [ANY] * 4,
        out_specs=(VM,) * 5,
        scratch_shapes=OUT_PLACE,
        cost_estimate=pl.CostEstimate(flops=2 * 8192 * 256 * 256, bytes_accessed=5 << 20, transcendentals=0),
    )(idx, rows, prod, gated, *pieces)


def combined(idx_here, count, span, rate, pieces):
    before, total = 0.0, 0.0
    for q in range(count):
        v = pieces[q].astype(F32)
        gap = (idx_here - 1 - q).astype(F32)
        w = jnp.where(gap >= 0, jnp.exp(-rate * (span * jnp.maximum(gap, 0.0))), 0.0)
        before = before + w * v
        total = total + jnp.exp(-rate * (span * float(count - 1 - q))) * v
    return before, total


def row_kernel(idx, rate, ends, before, total):
    b, t = combined(idx[2], 8, 256.0, rate[...], ends)
    before[...] = b
    for k in range(4):
        total[k] = t.astype(BF)


def row_states(idx, rate, ends):
    return pl.pallas_call(
        row_kernel,
        out_shape=(jax.ShapeDtypeStruct((2, 16, 256), F32), jax.ShapeDtypeStruct((4, 2, 16, 256), BF)),
        in_specs=[SM, VM, VM],
        out_specs=(VM, VM),
    )(idx, rate, ends)


def long_kernel(idx, gate, within, rate, before, totals, starts, gated, mine, theirs):
    r = rate[...]
    y, z = idx[1].astype(F32), idx[2].astype(F32)
    b, t = combined(idx[1], 4, 2048.0, r, totals)
    carry = jnp.exp(-r * (2048.0 * y))
    decay = jnp.exp(-r * (256.0 * z))
    entering = [before[0] + decay * b[0], before[1] + decay * (b[1] + carry * t[0])]
    lane = lax.broadcasted_iota(jnp.int32, (16, 256), 1) // GROUP
    for h in range(2):
        spread = jnp.concatenate([jnp.where(lane == k, entering[h], 0.0) for k in range(16)], axis=0)
        carried = jnp.dot(starts[...], spread.astype(BF), preferred_element_type=F32)
        gated[h] = (gate[h] * (within[h] + carried)).astype(BF)
    mine[...] = gated[idx[0]].T
    theirs[...] = gated[1 - idx[0]].T


def long_gated(idx, gate, within, rate, before, totals, starts):
    return pl.pallas_call(
        long_kernel,
        out_shape=(GATED, SQUARE, SQUARE),
        in_specs=[SM] + [VM] * 6,
        out_specs=(VM,) * 3,
        cost_estimate=pl.CostEstimate(flops=2 * 512 * 256 * 256, bytes_accessed=2 << 20, transcendentals=0),
    )(idx, gate, within, rate, before, totals, starts)


def slide_kernel(idx, mr, rates, residues, medium, local, taps, lags):
    here = pl.ds(pl.multiple_of(idx[0] * 16, 16), 16)
    turn = lax.broadcasted_iota(jnp.int32, (TAPS, 256), 0) + lax.broadcasted_iota(jnp.int32, (TAPS, 256), 1)
    taps[...] = jnp.dot(mr[here, :], jnp.where(turn == TAPS, 1.0, 0.0).astype(BF), preferred_element_type=F32)
    rate, residue = rates[here, :], residues[here, :]
    weight = residue * jnp.sqrt(2.0 * rate)
    lane = lax.broadcasted_iota(jnp.int32, (16, 256), 1)
    lag = jnp.where(lane == 0, 0, 256 - lane).astype(F32)
    total = jnp.zeros((16, 256), F32)
    for m in range(16):
        total = total + weight[:, m : m + 1] * jnp.exp(-rate[:, m : m + 1] * lag)
    lags[...] = total
    row = lax.broadcasted_iota(jnp.int32, (256, 256), 0)
    col = lax.broadcasted_iota(jnp.int32, (256, 256), 1)

    def group(k, carry):
        wide = jnp.broadcast_to(taps[pl.ds(k, 1), :], (TAPS, 256))
        medium[k] = pltpu.roll(wide, 0, 1, stride=1, stride_axis=0).astype(BF)
        wide = jnp.broadcast_to(lags[pl.ds(k, 1), :], (256, 256))
        turned = pltpu.roll(wide, 0, 1, stride=1, stride_axis=0)
        local[k] = jnp.where(col <= row, turned, 0.0).astype(BF)
        return carry

    lax.fori_loop(0, 16, group, 0)


def slide_filters(idx, mr, rates, residues):
    return pl.pallas_call(
        slide_kernel,
        out_shape=(
            jax.ShapeDtypeStruct((16, TAPS, 256), BF),
            jax.ShapeDtypeStruct((16, 256, 256), BF),
        ),
        in_specs=[SM, VM, VM, VM],
        out_specs=(VM,) * 2,
        scratch_shapes=[pltpu.VMEM((16, 256), F32), pltpu.VMEM((16, 256), F32)],
    )(idx, mr, rates, residues)


def gather_tokens(block):
    return [block] + [ring_shift(block, d) for d in (1, -1, 2)]


def reduced(before, here, w_here, w_there):
    there = flip(here, "co", 1)
    summed = out_sums(here, there, w_here, w_there)
    parts = exchange(summed, RING).astype(F32)
    return (before.astype(F32) + ((parts[0] + parts[1]) + (parts[2] + parts[3]))).astype(BF)


def placed(mine, got, half):
    return jnp.concatenate([jnp.where(half == 0, mine, got), jnp.where(half == 0, got, mine)], axis=0)


def modes_of(li_rate, li_residue, half):
    def part(v):
        n = v.shape[0] // 2
        return lax.dynamic_slice_in_dim(v, half * n, n, 0)

    rate, residue = part(li_rate), part(li_residue)
    weight = residue * jnp.sqrt(2.0 * rate)
    offs = jnp.arange(256, dtype=F32)
    flat = rate.reshape(256)
    ends_w = jnp.exp(-flat[:, None] * (255.0 - offs)).astype(BF)
    starts = (weight.reshape(256) * jnp.exp(-flat * (offs[:, None] + 1.0))).astype(BF)
    rate_mc = jnp.repeat(rate.T, GROUP, axis=1)
    return ends_w, starts, rate_mc


def both_operators(hidden, gain_a, in_a, mr_filter, out_a, gain_b, in_b, li_rate, li_residue, out_b):
    half = lax.axis_index("xh")
    idx = jnp.stack([lax.axis_index(a) for a in ("xh", "y", "z", "xl", "co")]).astype(jnp.int32)
    pieces_a = gather_first(*column_halves(in_a, out_a, half))
    ahead = lax.ppermute(hidden[TAPS:], CTX, [(i, i + 1) for i in range(63)])
    toks = gather_tokens(jnp.concatenate([ahead, hidden], axis=0))
    every = jnp.stack(toks)
    toks = toks + [flip(every, "co", 1)]
    ends_w, starts, rate_mc = modes_of(li_rate, li_residue, half)
    ins_b, outs_b = gather_second(*column_halves(in_b, out_b, half))

    normed = norm_rows(idx, gain_a, toks)
    medium_rows, local_rows = slide_filters(idx, mr_filter, li_rate, li_residue)
    gated_a, w_here, w_away = first_gated(idx, normed, medium_rows, pieces_a)
    w_there = flip(w_away, "co", 1)
    after_a = reduced(hidden, gated_a, w_here, w_there)

    toks = gather_tokens(after_a)
    near = flip(jnp.stack(toks[1:3]), "co", 1)
    toks = toks + [flip(toks[0], "co", 1), near, flip(toks[3], "co", 1)]
    gate, prod, ends = second_in(idx, gain_b, ends_w, toks, ins_b)
    by_z = exchange(ends, "z")
    within, mine_a, theirs_a, w_here, w_away = within_block(idx, local_rows, prod, gated_a, outs_b)
    w_there = flip(w_away, "co", 1)
    before, total = row_states(idx, rate_mc, by_z)
    by_y = exchange(total, "y")
    gated_b, mine, theirs = long_gated(idx, gate, within, rate_mc, before, by_y, starts)
    mixed = reduced(after_a, gated_b, w_here, w_there)
    got = shift(jnp.stack([theirs_a, theirs]), "xh", 1)
    gated_medium = placed(mine_a, got[0], half)
    gated_long = placed(mine, got[1], half)
    return mixed, gated_medium, gated_long


def solution(mesh):
    split = Mesh(mesh.devices.reshape(2, 4, 8, 2, 2), ("xh", "y", "z", "xl", "co"))
    in_specs = (
        P(CTX, TP),
        P(),
        P(None, CTX, TP),
        P(TP, None),
        P(TP, CTX),
        P(),
        P(None, CTX, TP),
        P(TP, None),
        P(TP, None),
        P(TP, CTX),
    )
    out_specs = (P(CTX, TP), P(TP, CTX), P(TP, CTX))
    return jax.shard_map(both_operators, mesh=split, in_specs=in_specs, out_specs=out_specs, check_vma=False)
```
